512 devices in a mesh: pair: 64 (over z, x), virt: 8 (over y, core).
Axes of the slice: x: 4, y: 4, z: 16, core: 2. Of those that a mesh axis runs over, the one named last changes fastest.
Arguments:
- amplitudes: bfloat16 [256, 1024, 1024], P('pair', None, 'virt'), may hold values from -0.1796875 to 0.1796875
- cholesky: bfloat16 [8, 1024, 1792], P(None, 'virt', 'pair'), may hold values from -0.1640625 to 0.1640625
- energy_first: float32 [32], replicated, may hold values from -3 to -0.3
- energy_second: float32 [8], replicated, may hold values from -3 to -0.3
- energy_virtual: float32 [1024], replicated, may hold values from 0.2 to 4
Outputs:
- residual: bfloat16 [256, 1024, 1024], P('pair', None, 'virt')
The draws below stay inside these ranges and needn't reach their ends.
All inputs are finite; a program needn't handle non-finite values.
Results may differ from the reference program's by a relative error of at most 0.0095.
Values may be sent and summed in bfloat16 or wider, within the bound.
A program may use at most 64 MiB of HBM per device.

```python
import jax
import jax.numpy as jnp
from jax import lax

OCC = 8
VIRT = 1024
NCHOL = 1792
PAIR_DEV = 4
PAIRS = 256
OCC_ROWS = 32
N_VIRT = 8


def block_levels(stream_key, extent, split, least, high):
    loudness = 1.0
    for position, blocks in split:
        steps = jax.random.uniform(jax.random.fold_in(jax.random.fold_in(stream_key, 6), position), (blocks,), jnp.float32, least / len(split), high / len(split))
        loudness = loudness * jnp.repeat(jnp.exp(steps), extent[position] // blocks).reshape((-1,) + (1,) * (len(extent) - 1 - position))
    return loudness


def normal_values(own_key, extent, width, most, split=(), kind=jnp.bfloat16):
    drawn = width * jax.random.normal(own_key, extent, jnp.float32)
    if split:
        drawn = drawn * block_levels(own_key, extent, split, -0.22, 0.18)
    return jnp.clip(drawn, -most, most).astype(kind)


def setup_inputs(seed: int = 0) -> dict:
    streams_of = jax.random.split(jax.random.key(seed), 6)
    return {
        "amplitudes": normal_values(streams_of[0], (PAIRS, VIRT, VIRT), 0.03, 0.1796875, ((0, 64), (2, 8))),
        "cholesky": normal_values(streams_of[1], (OCC, VIRT, NCHOL), (1.7 * (OCC * VIRT * NCHOL) ** -0.25), 0.1640625, ((1, 8), (2, 64))),
        "energy_first": jnp.clip(jax.random.uniform(streams_of[2], (OCC_ROWS,), jnp.float32, -3.0, -0.3), -3.0, -0.3),
        "energy_second": jnp.clip(jax.random.uniform(streams_of[3], (OCC,), jnp.float32, -3.0, -0.3), -3.0, -0.3),
        "energy_virtual": jnp.clip(jax.random.uniform(streams_of[4], (VIRT,), jnp.float32, 0.2, 4.0), 0.2, 4.0),
    }


def reference(amplitudes, cholesky, energy_first, energy_second, energy_virtual):
    vectors = cholesky.astype(jnp.float32)
    group_width = min(PAIR_DEV, OCC)
    group_count = OCC // group_width
    tile_width = VIRT // N_VIRT
    split_vectors = vectors.reshape(group_count, group_width, N_VIRT, tile_width, NCHOL)
    blocks = amplitudes.reshape(OCC_ROWS, OCC, VIRT, VIRT)
    virtual_pairs = energy_virtual[:, None] + energy_virtual[None, :]

    def one_row(inputs):
        block, first_energy = inputs
        values = block.astype(jnp.float32)
        combined = (2.0 * values - jnp.swapaxes(values, 1, 2)).astype(jnp.bfloat16)
        combined = lax.optimization_barrier(combined).astype(jnp.float32)
        split_combined = combined.reshape(group_count, group_width, VIRT, N_VIRT, tile_width)
        terms = jnp.einsum("gsatd,gstdq->gtaq", split_combined, split_vectors)
        terms = lax.optimization_barrier(terms.astype(jnp.bfloat16)).astype(jnp.float32)
        tile_sum = jnp.sum(terms, axis=1)
        tile_sum = lax.optimization_barrier(tile_sum.astype(jnp.bfloat16)).astype(jnp.float32)
        middle = jnp.sum(tile_sum, axis=0)
        middle = lax.optimization_barrier(middle.astype(jnp.bfloat16)).astype(jnp.float32)
        cycle_term = jnp.einsum("aq,lbq->lab", middle, vectors)
        diagonal = virtual_pairs[None, :, :] - first_energy - energy_second[:, None, None]
        return (diagonal * values + cycle_term).astype(jnp.bfloat16)

    results = lax.map(one_row, (blocks, energy_first))
    return results.reshape(OCC_ROWS * OCC, VIRT, VIRT)
```

```python
import jax
import jax.numpy as jnp
from jax import lax
from jax.experimental import pallas as pl
from jax.experimental.pallas import tpu as pltpu
from jax.sharding import PartitionSpec as P

MESH = pl.DeviceIdType.MESH
BF = jnp.bfloat16
F32 = jnp.float32
NZ, NX, NY = 16, 4, 4
TILE = 128
BLOCK = 112
SHARE = 28
CHUNKS = 8
FORMS = "EGEGEGEG"


def kernel(amp, vec, e_first, e_second, e_virtual, out,
           xg, lay, ltb, pbuf, b2, comb, tbuf, r1, s2, r2, inter, acc, away,
           xs, xr, ps, pr, ys, yr, zs, zr, cs, cr, g1s, g1r, g2s, g2r, g3s, g3r, g4s, g4r, os_, or_):
    p = lax.axis_index("pair")
    v = lax.axis_index("virt")
    z, x, y, c = p // NX, p % NX, v // 2, v % 2
    xo = x % 2
    xp = x + 1 - 2 * xo

    def dev(z=z, x=x, y=y, c=c):
        return (z * NX + x, y * 2 + c)

    core = dev(c=1 - c)
    across = dev(x=xp)
    y_up = [None] + [dev(y=(y + r) % NY) for r in range(1, NY)]
    y_down = [None] + [dev(y=(y + NY - r) % NY) for r in range(1, NY)]
    x_up = [None] + [dev(x=(x + r) % NX) for r in range(1, NX)]
    z_up = dev(z=(z + 1) % NZ)
    z_down = dev(z=(z + NZ - 1) % NZ)

    started = []

    def send(src, dst, ssem, rsem, target):
        copy = pltpu.make_async_remote_copy(
            src_ref=src, dst_ref=dst, send_sem=ssem, recv_sem=rsem, device_id=target, device_id_type=MESH
        )
        copy.start()
        started.append(copy)
        return copy

    barrier = pltpu.get_barrier_semaphore()
    partners = [core, *y_up[1:], *x_up[1:], z_up, z_down]
    for partner in partners:
        pl.semaphore_signal(barrier, inc=1, device_id=partner, device_id_type=MESH)
    pl.semaphore_wait(barrier, len(partners))

    x_copies = []
    for r in range(1, NX):
        to = (x + r) % NX
        x_copies.append(send(vec.at[to % 2], xg.at[x], xs.at[r - 1], xr.at[r - 1], x_up[r]))
    p_copy = send(amp.at[:, :, 1 - c], pbuf, ps.at[0], pr.at[0], core)
    y_copies = [None] * NY
    for r in (1, 3, 2):
        y_copies[r] = send(amp.at[:, (y + r) % NY], b2.at[r - 1], ys.at[r - 1], yr.at[r - 1], y_up[r])

    xg[x] = vec[xo]
    for copy in x_copies:
        copy.wait_recv()
    for j in range(4):
        for k in range(NX):
            lay[j, SHARE * k : SHARE * (k + 1), :] = xg[k].astype(F32)[SHARE * j : SHARE * (j + 1), :]
    for j in range(4):
        ltb[0, 0, j] = lay[j].astype(BF)

    z_copies = {}
    c_copies = {}

    def share(slot):
        for u in range(2):
            part = pl.ds(2 * u, 2)
            c_copies[slot, u] = send(
                ltb.at[slot, 0, part], ltb.at[slot, 1, part], cs.at[slot, u], cr.at[slot, u], core
            )

    def ring(step):
        for u in range(2):
            part = pl.ds(2 * u, 2)
            if step <= 8:
                z_copies[0, step, u] = send(
                    ltb.at[step - 1, 0, part], ltb.at[step, 0, part],
                    zs.at[0, step - 1, u], zr.at[0, step - 1, u], z_down,
                )
            if step <= 7:
                z_copies[1, step, u] = send(
                    ltb.at[(NZ + 1 - step) % NZ, 0, part], ltb.at[NZ - step, 0, part],
                    zs.at[1, step - 1, u], zr.at[1, step - 1, u], z_up,
                )

    def service(step):
        for u in range(2):
            for way in range(2):
                if (way, step, u) in z_copies:
                    z_copies[way, step, u].wait_recv()
        if step < 8:
            ring(step + 1)
        share(step)
        if step <= 7:
            share(NZ - step)

    ring(1)
    share(0)

    p_copy.wait_recv()

    def turn(r):
        at = (y + NY - r) % NY
        for l in range(4):
            for s in range(2):
                block = amp[l, at, c] if s == 0 else pbuf[l, at]
                comb[pl.ds((2 * l + s) * TILE, TILE), pl.ds(r * TILE, TILE)] = block.T

    def mirror(r):
        for l in range(4):
            for s in range(2):
                half = c if s == 0 else 1 - c
                rows, cols = pl.ds((2 * l + s) * TILE, TILE), pl.ds(r * TILE, TILE)
                other = amp[l, y, half] if r == 0 else b2[r - 1, l, half]
                comb[rows, cols] = (2.0 * comb[rows, cols].astype(F32) - other.astype(F32)).astype(BF)

    turn(0)
    turn(1)
    service(1)
    turn(2)
    turn(3)
    service(2)
    mirror(0)
    service(3)
    for r in (1, 3):
        y_copies[r].wait_recv()
        mirror(r)
    service(4)
    y_copies[2].wait_recv()
    mirror(2)

    def vectors_of(slot):
        return jnp.concatenate([ltb[slot, s, j] for j in range(4) for s in range(2)], axis=1)

    one, two, three, four = {}, {}, {}, {}

    def stage_one(k):
        slots = ((NZ - k) % NZ, k + 1)
        for slot in slots:
            for u in range(2):
                c_copies[slot, u].wait_recv()
        for half, slot in enumerate(slots):
            term = jnp.dot(vectors_of(slot), comb[...], preferred_element_type=F32).astype(BF)
            for r in range(NY):
                tbuf[k, half, r] = term[:, r * TILE : (r + 1) * TILE]
        if FORMS[k] == "E":
            one[k] = [send(tbuf.at[k, 1 - xo], r1.at[k, pl.ds(0, 4)], g1s.at[k, 0], g1r.at[k, 0], across)]
        else:
            one[k] = [
                send(tbuf.at[k, :, r], r1.at[k, pl.ds(2 * (r - 1), 2)], g1s.at[k, r - 1], g1r.at[k, r - 1], y_down[r])
                for r in range(1, NY)
            ]

    def stage_two(k):
        for copy in one[k]:
            copy.wait_recv()
        if FORMS[k] == "E":
            for r in (1, 2, 3, 0):
                s2[k, r] = (tbuf[k, xo, r].astype(F32) + r1[k, r].astype(F32)).astype(BF)
            two[k] = [
                send(s2.at[k, r], r2.at[k, r - 1], g2s.at[k, r - 1], g2r.at[k, r - 1], y_down[r])
                for r in range(1, NY)
            ]
        else:
            for h in range(2):
                total = tbuf[k, h, 0].astype(F32)
                for r in range(1, NY):
                    total = total + r1[k, 2 * (r - 1) + h].astype(F32)
                s2[k, h] = total.astype(BF)
            two[k] = [send(s2.at[k, 1 - xo], r2.at[k, 0], g2s.at[k, 0], g2r.at[k, 0], across)]

    def stage_three(k):
        for copy in two[k]:
            copy.wait_recv()
        if FORMS[k] == "E":
            total = s2[k, 0].astype(F32)
            for r in range(1, NY):
                total = total + r2[k, r - 1].astype(F32)
            inter[k, xo, 0] = total.astype(BF)
            three[k] = [
                send(inter.at[k, xo, 0], inter.at[k, xo, r], g3s.at[k, r - 1], g3r.at[k, r - 1], y_up[r])
                for r in range(1, NY)
            ]
        else:
            inter[k, xo, 0] = (s2[k, xo].astype(F32) + r2[k, 0].astype(F32)).astype(BF)
            three[k] = [send(inter.at[k, xo, 0], inter.at[k, xo, 0], g3s.at[k, 0], g3r.at[k, 0], across)]

    def stage_four(k):
        for copy in three[k]:
            copy.wait_recv()
        if FORMS[k] == "E":
            four[k] = [send(inter.at[k, xo], inter.at[k, xo], g4s.at[k, 0], g4r.at[k, 0], across)]
        else:
            four[k] = [
                send(inter.at[k, :, 0], inter.at[k, :, r], g4s.at[k, r - 1], g4r.at[k, r - 1], y_up[r])
                for r in range(1, NY)
            ]

    def finish(k):
        for copy in four[k]:
            copy.wait_recv()
        slots = ((NZ - k) % NZ, k + 1)
        pad = jnp.zeros((256 - 2 * BLOCK, TILE), BF)
        left = jnp.concatenate(
            [jnp.concatenate([inter[k, 0, r], inter[k, 1, r], pad], axis=0).T for r in range(NY)], axis=0
        )
        wide = jnp.zeros((256 - 2 * BLOCK, 8 * TILE), BF)
        right = jnp.concatenate([vectors_of(slots[0]), vectors_of(slots[1]), wide], axis=0)
        product = jnp.dot(left, right, preferred_element_type=F32)
        if k == 0:
            acc[...] = product
        else:
            acc[...] += product

    for tick in range(CHUNKS + 4):
        if 0 <= tick - 1 < CHUNKS:
            stage_two(tick - 1)
        if 0 <= tick - 2 < CHUNKS:
            stage_three(tick - 2)
        if 0 <= tick - 3 < CHUNKS:
            stage_four(tick - 3)
        if tick < CHUNKS:
            stage_one(tick)
        if 5 <= tick + 5 <= 8:
            service(tick + 5)
        if 0 <= tick - 4 < CHUNKS:
            finish(tick - 4)

    turned = e_virtual[...].T
    first = e_first[p // 2]
    sides = []
    for r in range(NY):
        at = (y + NY - r) % NY
        column = jnp.where(c == 0, turned[:, 0:1], turned[:, 1:2])
        for q in range(1, NY):
            choice = jnp.where(c == 0, turned[:, 2 * q : 2 * q + 1], turned[:, 2 * q + 1 : 2 * q + 2])
            column = jnp.where(at == q, choice, column)
        sides.append(column)
    o_copies = []
    for s in (1, 0):
        half = c if s == 0 else 1 - c
        tops = e_virtual[pl.ds(2 * y + half, 1), :]
        for l in range(4):
            second = e_second[4 * xo + l]
            for r in range(NY):
                at = (y + NY - r) % NY
                values = (amp[l, at, c] if s == 0 else pbuf[l, at]).astype(F32)
                term = acc[r * TILE : (r + 1) * TILE, (2 * l + s) * TILE : (2 * l + s + 1) * TILE]
                result = ((sides[r] + tops - first - second) * values + term).astype(BF)
                if s == 0:
                    out[l, at, c] = result
                else:
                    away[l, at] = result
            if s == 1:
                o_copies.append(send(away.at[l], out.at[l, :, c], os_.at[l], or_.at[l], core))
    for copy in o_copies:
        copy.wait_recv()
    for copy in started:
        copy.wait_send()


def on_device(amplitudes, cholesky, energy_first, energy_second, energy_virtual):
    amp = amplitudes.reshape(4, NY, 2, TILE, TILE)
    vec = jnp.transpose(cholesky, (0, 2, 1)).reshape(2, 4 * SHARE, TILE)
    vmem = pl.BlockSpec(memory_space=pltpu.VMEM)
    smem = pl.BlockSpec(memory_space=pltpu.SMEM)
    dma = pltpu.SemaphoreType.DMA
    scratch = [
        pltpu.VMEM((NX, 4 * SHARE, TILE), BF),
        pltpu.VMEM((4, BLOCK, TILE), F32),
        pltpu.VMEM((NZ, 2, 4, BLOCK, TILE), BF),
        pltpu.VMEM((4, NY, TILE, TILE), BF),
        pltpu.VMEM((NY - 1, 4, 2, TILE, TILE), BF),
        pltpu.VMEM((8 * TILE, NY * TILE), BF),
        pltpu.VMEM((CHUNKS, 2, NY, BLOCK, TILE), BF),
        pltpu.VMEM((CHUNKS, 6, BLOCK, TILE), BF),
        pltpu.VMEM((CHUNKS, 4, BLOCK, TILE), BF),
        pltpu.VMEM((CHUNKS, 3, BLOCK, TILE), BF),
        pltpu.VMEM((CHUNKS, 2, NY, BLOCK, TILE), BF),
        pltpu.VMEM((NY * TILE, 8 * TILE), F32),
        pltpu.VMEM((4, NY, TILE, TILE), BF),
        dma((3,)), dma((3,)), dma((1,)), dma((1,)), dma((3,)), dma((3,)),
        dma((2, 8, 2)), dma((2, 8, 2)), dma((NZ, 2)), dma((NZ, 2)),
        *[dma((CHUNKS, 3)) for _ in range(8)],
        dma((4,)), dma((4,)),
    ]
    result = pl.pallas_call(
        kernel,
        out_shape=jax.ShapeDtypeStruct(amp.shape, BF),
        in_specs=[vmem, vmem, smem, smem, vmem],
        out_specs=vmem,
        scratch_shapes=scratch,
        compiler_params=pltpu.CompilerParams(collective_id=0, has_side_effects=True, vmem_limit_bytes=48 << 20),
        name="cycle",
    )(amp, vec, energy_first, energy_second, energy_virtual.reshape(8, TILE))
    return result.reshape(amplitudes.shape)


def solution(mesh):
    placed = (P("pair", None, "virt"), P(None, "virt", "pair"), P(), P(), P())
    return jax.shard_map(
        on_device, mesh=mesh, in_specs=placed, out_specs=P("pair", None, "virt"), check_vma=False
    )
```

```python
import jax
import jax.numpy as jnp
from jax import lax
from jax.experimental import pallas as pl
from jax.experimental.pallas import tpu as pltpu
from jax.sharding import PartitionSpec as P

MESH = pl.DeviceIdType.MESH
BF = jnp.bfloat16
F32 = jnp.float32
NZ, NX, NY = 16, 4, 4
TILE = 128
BLOCK = 112
SHARE = 28
CHUNKS = 8
FORMS = "EGEGEGDD"
ROWS = ((0, 64), (64, 48))
LAG = 3


def kernel(amp, vec, e_first, e_second, e_virtual, out,
           own, tops_of, xg, lay, ltb, pbuf, b2, comb, tbuf, r1, s2, r2, inter, acc, away,
           lsem, xs, xr, ps, pr, ys, yr, zs, zr, cs, cr, gs, gr, os_, or_):
    p = lax.axis_index("pair")
    v = lax.axis_index("virt")
    z, x, y, c = p // NX, p % NX, v // 2, v % 2
    xo = x % 2
    xp = x + 1 - 2 * xo

    def dev(z=z, x=x, y=y, c=c):
        return (z * NX + x, y * 2 + c)

    core = dev(c=1 - c)
    across = dev(x=xp)
    y_up = [None] + [dev(y=(y + r) % NY) for r in range(1, NY)]
    y_down = [None] + [dev(y=(y + NY - r) % NY) for r in range(1, NY)]
    x_up = [None] + [dev(x=(x + r) % NX) for r in range(1, NX)]
    z_up = dev(z=(z + 1) % NZ)
    z_down = dev(z=(z + NZ - 1) % NZ)

    y_slant = [across] + [dev(x=xp, y=(y + r) % NY) for r in range(1, NY)]
    y_slope = [across] + [dev(x=xp, y=(y + NY - r) % NY) for r in range(1, NY)]

    def send(src, dst, ssem, rsem, target):
        copy = pltpu.make_async_remote_copy(
            src_ref=src, dst_ref=dst, send_sem=ssem, recv_sem=rsem, device_id=target, device_id_type=MESH
        )
        copy.start()
        return copy

    def whole(ref, ssem, rsem):
        return pltpu.make_async_remote_copy(
            src_ref=ref, dst_ref=ref, send_sem=ssem, recv_sem=rsem, device_id=core, device_id_type=MESH
        )

    local = [
        pltpu.make_async_copy(amp, own, lsem.at[0]),
        pltpu.make_async_copy(e_virtual, tops_of, lsem.at[1]),
    ]
    for copy in local:
        copy.start()

    barrier = pltpu.get_barrier_semaphore()
    partners = [core, *y_up[1:], *x_up[1:], z_up, z_down, *y_slant[1:]]

    def enter():
        for partner in partners:
            pl.semaphore_signal(barrier, inc=1, device_id=partner, device_id_type=MESH)
        pl.semaphore_wait(barrier, len(partners))

    enter()

    for r in range(1, NX):
        to = (x + r) % NX
        send(vec.at[to % 2], xg.at[x], xs.at[0], xr.at[0], x_up[r])
    p_copy = send(amp.at[:, :, 1 - c], pbuf, ps.at[0], pr.at[0], core)
    y_copies = [None] * NY
    for r in (1, 3, 2):
        y_copies[r] = send(amp.at[:, (y + r) % NY], b2.at[r - 1], ys.at[0], yr.at[r - 1], y_up[r])
    xg[x] = vec[xo]
    x_all = whole(xg.at[pl.ds(0, NX - 1)], xs.at[0], xr.at[0])
    y_all = whole(b2, ys.at[0], yr.at[0])

    def arrive(copies):
        for copy in copies:
            copy.wait_recv()

    def spread():
        for j in range(4):
            for k in range(NX):
                lay[j, SHARE * k : SHARE * (k + 1), :] = xg[k].astype(F32)[SHARE * j : SHARE * (j + 1), :]

    arrive([x_all])
    spread()

    z_copies = {}
    pending = {}

    def settle(key):
        if key in pending:
            pending.pop(key).wait_send()

    def share(way, step, u):
        slot = step if way == 0 else NZ - step
        key = ("c", way, step % 2)
        if u == 0:
            settle(key)
        sem = cs.at[way, step % 2]
        send(ltb.at[slot, 0, u], ltb.at[slot, 1, u], sem, cr.at[slot], core)
        pending[key] = whole(ltb.at[slot, 0], sem, cr.at[slot])

    def ring(step, way, u):
        if step > 8 - way:
            return
        source = step - 1 if way == 0 else (NZ + 1 - step) % NZ
        target = step if way == 0 else NZ - step
        key = ("z", way, step % 2)
        if u == 0:
            settle(key)
        sem = zs.at[way, step % 2]
        z_copies[way, step, u] = send(
            ltb.at[source, 0, u], ltb.at[target, 0, u], sem, zr.at[way, step - 1, u], z_up if way else z_down
        )
        pending[key] = whole(ltb.at[source, 0], sem, zr.at[way, step - 1, u])

    def relay(step, u):
        for way in range(2):
            if (way, step, u) in z_copies:
                z_copies[way, step, u].wait_recv()
                ring(step + 1, way, u)
                share(way, step, u)

    def service(step):
        for u in range(4):
            relay(step, u)

    for j in range(4):
        ltb[0, 0, j] = lay[j].astype(BF)
        ring(1, 0, j)
        ring(1, 1, j)
        share(0, 0, j)

    for copy in local:
        copy.wait()
    arrive([p_copy])

    def turn(r):
        at = (y + NY - r) % NY
        for l in range(4):
            for s in range(2):
                block = own[l, at, c] if s == 0 else pbuf[l, at]
                comb[pl.ds((2 * l + s) * TILE, TILE), pl.ds(r * TILE, TILE)] = block.T

    def mirror(r):
        for l in range(4):
            for s in range(2):
                half = c if s == 0 else 1 - c
                rows, cols = pl.ds((2 * l + s) * TILE, TILE), pl.ds(r * TILE, TILE)
                other = own[l, y, half] if r == 0 else b2[r - 1, l, half]
                comb[rows, cols] = (2.0 * comb[rows, cols].astype(F32) - other.astype(F32)).astype(BF)

    turn(0)
    turn(1)
    service(1)
    turn(2)
    turn(3)
    mirror(0)
    service(2)
    for r in (1, 3, 2):
        arrive([y_copies[r]])
        mirror(r)

    def vectors_of(slot):
        return jnp.concatenate([ltb[slot, s, j] for j in range(4) for s in range(2)], axis=1)

    landed = {}

    def post(stage, n, region, copies):
        key = (stage, n % 4)
        settle(key)
        ssem, rsem = gs.at[stage, n % 4], gr.at[stage, n]
        for src, dst, target in copies:
            send(src, dst, ssem, rsem, target)
        pending[key] = landed[stage, n] = whole(region, ssem, rsem)

    def rows_of(n):
        return n // 2, pl.ds(*ROWS[n % 2])

    def stage_one(k):
        slots = ((NZ - k) % NZ, k + 1)
        for slot in slots:
            whole(ltb.at[slot, 1], cs.at[0, 0], cr.at[slot]).wait_recv()
        for half, slot in enumerate(slots):
            term = jnp.dot(vectors_of(slot), comb[...], preferred_element_type=F32).astype(BF)
            for r in range(NY):
                tbuf[k, half, r] = term[:, r * TILE : (r + 1) * TILE]
        for n in (2 * k, 2 * k + 1):
            _, rows = rows_of(n)
            if FORMS[k] == "E":
                post(0, n, r1.at[k, pl.ds(0, 4), rows],
                     [(tbuf.at[k, 1 - xo, :, rows], r1.at[k, pl.ds(0, 4), rows], across)])
            elif FORMS[k] == "G":
                post(0, n, r1.at[k, pl.ds(0, 6), rows],
                     [(tbuf.at[k, :, r, rows], r1.at[k, pl.ds(2 * (r - 1), 2), rows], y_down[r]) for r in (2, 1, 3)])
            else:
                post(0, n, r1.at[k, :, rows],
                     [(tbuf.at[k, 1 - xo, r, rows], r1.at[k, 3 + r, rows], y_slope[r]) for r in (2, 1, 3, 0)]
                     + [(tbuf.at[k, xo, r, rows], r1.at[k, r - 1, rows], y_down[r]) for r in (2, 1, 3)])

    def stage_two(n):
        k, rows = rows_of(n)
        landed[0, n].wait_recv()
        if FORMS[k] == "E":
            for r in range(NY):
                s2[k, r, rows] = (tbuf[k, xo, r, rows].astype(F32) + r1[k, r, rows].astype(F32)).astype(BF)
            post(1, n, r2.at[k, :, rows],
                 [(s2.at[k, r, rows], r2.at[k, r - 1, rows], y_down[r]) for r in (2, 1, 3)])
        elif FORMS[k] == "G":
            for h in range(2):
                total = tbuf[k, h, 0, rows].astype(F32)
                for r in range(1, NY):
                    total = total + r1[k, 2 * (r - 1) + h, rows].astype(F32)
                s2[k, h, rows] = total.astype(BF)
            post(1, n, r2.at[k, 0, rows], [(s2.at[k, 1 - xo, rows], r2.at[k, 0, rows], across)])
        else:
            total = tbuf[k, xo, 0, rows].astype(F32)
            for q in range(7):
                total = total + r1[k, q, rows].astype(F32)
            inter[k, xo, 0, rows] = total.astype(BF)
            mine = inter.at[k, xo, 0, rows]
            post(3, n, inter.at[k, 1 - xo, :, rows],
                 [(mine, inter.at[k, xo, r, rows], y_slant[r]) for r in (2, 1, 3, 0)])
            post(2, n, inter.at[k, xo, pl.ds(1, 3), rows],
                 [(mine, inter.at[k, xo, r, rows], y_up[r]) for r in (2, 1, 3)])

    def stage_three(n):
        k, rows = rows_of(n)
        landed[1, n].wait_recv()
        if FORMS[k] == "E":
            total = s2[k, 0, rows].astype(F32)
            for r in range(1, NY):
                total = total + r2[k, r - 1, rows].astype(F32)
            inter[k, xo, 0, rows] = total.astype(BF)
            post(2, n, inter.at[k, xo, pl.ds(1, 3), rows],
                 [(inter.at[k, xo, 0, rows], inter.at[k, xo, r, rows], y_up[r]) for r in (2, 1, 3)])
        else:
            inter[k, xo, 0, rows] = (s2[k, xo, rows].astype(F32) + r2[k, 0, rows].astype(F32)).astype(BF)
            post(2, n, inter.at[k, 1 - xo, 0, rows],
                 [(inter.at[k, xo, 0, rows], inter.at[k, xo, 0, rows], across)])

    def stage_four(n):
        k, rows = rows_of(n)
        landed[2, n].wait_recv()
        if FORMS[k] == "E":
            post(3, n, inter.at[k, 1 - xo, :, rows],
                 [(inter.at[k, xo, :, rows], inter.at[k, xo, :, rows], across)])
        else:
            post(3, n, inter.at[k, :, pl.ds(1, 3), rows],
                 [(inter.at[k, :, 0, rows], inter.at[k, :, r, rows], y_up[r]) for r in (2, 1, 3)])

    def finish(k):
        for n in (2 * k, 2 * k + 1):
            if FORMS[k] == "D":
                landed[2, n].wait_recv()
            landed[3, n].wait_recv()
        slots = ((NZ - k) % NZ, k + 1)
        pad = jnp.zeros((256 - 2 * BLOCK, TILE), BF)
        left = jnp.concatenate(
            [jnp.concatenate([inter[k, 0, r], inter[k, 1, r], pad], axis=0).T for r in range(NY)], axis=0
        )
        wide = jnp.zeros((256 - 2 * BLOCK, 8 * TILE), BF)
        right = jnp.concatenate([vectors_of(slots[0]), vectors_of(slots[1]), wide], axis=0)
        product = jnp.dot(left, right, preferred_element_type=F32)
        if k == 0:
            acc[...] = product
        else:
            acc[...] += product

    plan = []
    for step in range(3, 9):
        for u in range(4):
            plan.append((2 * (step - 2) + 0.5 * u - 0.3, 9, relay, (step, u)))
    for k in range(CHUNKS):
        short = FORMS[k] == "D"
        plan.append((2 * k, 4, stage_one, (k,)))
        for n in (2 * k, 2 * k + 1):
            plan.append((n + LAG, 3, stage_two, (n,)))
            if not short:
                plan.append((n + 2 * LAG, 2, stage_three, (n,)))
                plan.append((n + 3 * LAG, 1, stage_four, (n,)))
        plan.append((2 * k + 1 + (2 if short else 4) * LAG, 5, finish, (k,)))
    for _, _, act, what in sorted(plan, key=lambda item: item[:2]):
        act(*what)

    def conclude():
        turned = tops_of[...].T
        first = e_first[p // 2]
        sides = []
        for r in range(NY):
            at = (y + NY - r) % NY
            column = jnp.where(c == 0, turned[:, 0:1], turned[:, 1:2])
            for q in range(1, NY):
                choice = jnp.where(c == 0, turned[:, 2 * q : 2 * q + 1], turned[:, 2 * q + 1 : 2 * q + 2])
                column = jnp.where(at == q, choice, column)
            sides.append(column)
        for s in (1, 0):
            half = c if s == 0 else 1 - c
            tops = tops_of[pl.ds(2 * y + half, 1), :]
            for l in range(4):
                second = e_second[4 * xo + l]
                for r in range(NY):
                    at = (y + NY - r) % NY
                    values = (own[l, at, c] if s == 0 else pbuf[l, at]).astype(F32)
                    term = acc[r * TILE : (r + 1) * TILE, (2 * l + s) * TILE : (2 * l + s + 1) * TILE]
                    result = ((sides[r] + tops - first - second) * values + term).astype(BF)
                    if s == 0:
                        out[l, at, c] = result
                    else:
                        away[l, at] = result
                if s == 1:
                    send(away.at[l], out.at[l, :, c], os_.at[0], or_.at[0], core)

    conclude()
    last = whole(away, os_.at[0], or_.at[0])
    arrive([last])

    def drain():
        for copy in (x_all, p_copy, y_all, last, *pending.values()):
            copy.wait_send()

    drain()


def on_device(amplitudes, cholesky, energy_first, energy_second, energy_virtual):
    amp = amplitudes.reshape(4, NY, 2, TILE, TILE)
    vec = jnp.transpose(cholesky, (0, 2, 1)).reshape(2, 4 * SHARE, TILE)
    vmem = pl.BlockSpec(memory_space=pltpu.VMEM)
    hbm = pl.BlockSpec(memory_space=pltpu.HBM)
    smem = pl.BlockSpec(memory_space=pltpu.SMEM)
    dma = pltpu.SemaphoreType.DMA
    scratch = [
        pltpu.VMEM((4, NY, 2, TILE, TILE), BF),
        pltpu.VMEM((8, TILE), F32),
        pltpu.VMEM((NX, 4 * SHARE, TILE), BF),
        pltpu.VMEM((4, BLOCK, TILE), F32),
        pltpu.VMEM((NZ, 2, 4, BLOCK, TILE), BF),
        pltpu.VMEM((4, NY, TILE, TILE), BF),
        pltpu.VMEM((NY - 1, 4, 2, TILE, TILE), BF),
        pltpu.VMEM((8 * TILE, NY * TILE), BF),
        pltpu.VMEM((CHUNKS, 2, NY, BLOCK, TILE), BF),
        pltpu.VMEM((CHUNKS, 7, BLOCK, TILE), BF),
        pltpu.VMEM((CHUNKS, 4, BLOCK, TILE), BF),
        pltpu.VMEM((CHUNKS, 3, BLOCK, TILE), BF),
        pltpu.VMEM((CHUNKS, 2, NY, BLOCK, TILE), BF),
        pltpu.VMEM((NY * TILE, 8 * TILE), F32),
        pltpu.VMEM((4, NY, TILE, TILE), BF),
        dma((2,)), dma((1,)), dma((1,)), dma((1,)), dma((1,)), dma((1,)), dma((3,)),
        dma((2, 2)), dma((2, 8, 4)), dma((2, 2)), dma((NZ,)),
        dma((4, 4)), dma((4, 2 * CHUNKS)), dma((1,)), dma((1,)),
    ]
    result = pl.pallas_call(
        kernel,
        out_shape=jax.ShapeDtypeStruct(amp.shape, BF),
        in_specs=[hbm, vmem, smem, smem, hbm],
        out_specs=vmem,
        scratch_shapes=scratch,
        compiler_params=pltpu.CompilerParams(collective_id=0, has_side_effects=True, vmem_limit_bytes=48 << 20),
        name="cycle",
    )(amp, vec, energy_first, energy_second, energy_virtual.reshape(8, TILE))
    return result.reshape(amplitudes.shape)


def solution(mesh):
    placed = (P("pair", None, "virt"), P(None, "virt", "pair"), P(), P(), P())
    return jax.shard_map(
        on_device, mesh=mesh, in_specs=placed, out_specs=P("pair", None, "virt"), check_vma=False
    )
```

```python
import jax
import jax.numpy as jnp
from jax import lax
from jax.experimental import pallas as pl
from jax.experimental.pallas import tpu as pltpu
from jax.sharding import PartitionSpec as P

MESH = pl.DeviceIdType.MESH
BF = jnp.bfloat16
F32 = jnp.float32
NZ, NX, NY = 16, 4, 4
TILE = 128
BLOCK = 112
SHARE = 28
CHUNKS = 8
FORMS = "EEGEEGED"
ROWS = ((0, 64), (64, 48))
LAG = 3
GRANT = 66_900_000


def kernel(amp, chol, first_hbm, second_hbm, virtual_hbm, out,
           own, tops_of, e_first, e_second, raw, wide_raw, flat, vec, xg, lay, ltb, pbuf, b2, comb, tbuf, r1, s2, r2, inter, acc, away, keep,
           lsem, xs, xr, ps, pr, ys, yr, zs, zr, cs, cr, gs, gr, os_, or_):
    p = lax.axis_index("pair")
    v = lax.axis_index("virt")
    z, x, y, c = p // NX, p % NX, v // 2, v % 2
    xo = x % 2
    xp = x + 1 - 2 * xo

    def dev(z=z, x=x, y=y, c=c):
        return (z * NX + x, y * 2 + c)

    core = dev(c=1 - c)
    across = dev(x=xp)
    y_up = [None] + [dev(y=(y + r) % NY) for r in range(1, NY)]
    y_down = [None] + [dev(y=(y + NY - r) % NY) for r in range(1, NY)]
    x_up = [None] + [dev(x=(x + r) % NX) for r in range(1, NX)]
    z_up = dev(z=(z + 1) % NZ)
    z_down = dev(z=(z + NZ - 1) % NZ)

    y_slant = [across] + [dev(x=xp, y=(y + r) % NY) for r in range(1, NY)]
    y_slope = [across] + [dev(x=xp, y=(y + NY - r) % NY) for r in range(1, NY)]

    def send(src, dst, ssem, rsem, target):
        copy = pltpu.make_async_remote_copy(
            src_ref=src, dst_ref=dst, send_sem=ssem, recv_sem=rsem, device_id=target, device_id_type=MESH
        )
        copy.start()
        return copy

    def whole(ref, ssem, rsem):
        return pltpu.make_async_remote_copy(
            src_ref=ref, dst_ref=ref, send_sem=ssem, recv_sem=rsem, device_id=core, device_id_type=MESH
        )

    local = [
        pltpu.make_async_copy(amp, own, lsem.at[0]),
        pltpu.make_async_copy(virtual_hbm, tops_of, lsem.at[1]),
        pltpu.make_async_copy(first_hbm, e_first, lsem.at[2]),
        pltpu.make_async_copy(second_hbm, e_second, lsem.at[3]),
    ]
    chol_copy = pltpu.make_async_copy(chol, raw, lsem.at[4])
    chol_copy.start()
    for copy in local:
        copy.start()

    barrier = pltpu.get_barrier_semaphore()
    partners = [core, *y_up[1:], *x_up[1:], z_up, z_down, *y_slant[1:]]

    def enter():
        for partner in partners:
            pl.semaphore_signal(barrier, inc=1, device_id=partner, device_id_type=MESH)
        chol_copy.wait()
        wide_raw[...] = raw[...].astype(F32)
        for j in range(4):
            for g in range(2):
                flat[g, SHARE * j : SHARE * (j + 1), :] = wide_raw[:, 4 * g + j, :]
        for g in range(2):
            vec[g] = flat[g].astype(BF)
        pl.semaphore_wait(barrier, len(partners))

    enter()

    for r in range(1, NX):
        to = (x + r) % NX
        send(vec.at[to % 2], xg.at[x], xs.at[0], xr.at[0], x_up[r])
    p_copy = send(amp.at[:, :, 1 - c], pbuf, ps.at[0], pr.at[0], core)
    y_copies = [None] * NY
    for r in (1, 3, 2):
        y_copies[r] = send(amp.at[:, (y + r) % NY], b2.at[r - 1], ys.at[0], yr.at[r - 1], y_up[r])
    xg[x] = vec[xo]
    x_all = whole(xg.at[pl.ds(0, NX - 1)], xs.at[0], xr.at[0])
    y_all = whole(b2, ys.at[0], yr.at[0])

    def arrive(copies):
        for copy in copies:
            copy.wait_recv()

    def spread():
        for j in range(4):
            for k in range(NX):
                lay[j, SHARE * k : SHARE * (k + 1), :] = xg[k].astype(F32)[SHARE * j : SHARE * (j + 1), :]

    arrive([x_all])
    spread()

    z_copies = {}
    pending = {}

    def settle(key):
        if key in pending:
            pending.pop(key).wait_send()

    def share(way, step, u):
        slot = step if way == 0 else NZ - step
        key = ("c", way, step % 2)
        if u == 0:
            settle(key)
        sem = cs.at[way, step % 2]
        send(ltb.at[slot, 0, u], ltb.at[slot, 1, u], sem, cr.at[slot], core)
        pending[key] = whole(ltb.at[slot, 0], sem, cr.at[slot])

    def ring(step, way, u):
        if step > 8 - way:
            return
        source = step - 1 if way == 0 else (NZ + 1 - step) % NZ
        target = step if way == 0 else NZ - step
        key = ("z", way, step % 2)
        if u == 0:
            settle(key)
        sem = zs.at[way, step % 2]
        z_copies[way, step, u] = send(
            ltb.at[source, 0, u], ltb.at[target, 0, u], sem, zr.at[way, step - 1, u], z_up if way else z_down
        )
        pending[key] = whole(ltb.at[source, 0], sem, zr.at[way, step - 1, u])

    def relay(step, u):
        for way in range(2):
            if (way, step, u) in z_copies:
                z_copies[way, step, u].wait_recv()
                ring(step + 1, way, u)
                share(way, step, u)

    def service(step):
        for u in range(4):
            relay(step, u)

    for j in range(4):
        ltb[0, 0, j] = lay[j].astype(BF)
        ring(1, 0, j)
        ring(1, 1, j)
        share(0, 0, j)

    for copy in local:
        copy.wait()
    arrive([p_copy])

    def turn(r):
        at = (y + NY - r) % NY
        for l in range(4):
            for s in range(2):
                block = own[l, at, c] if s == 0 else pbuf[l, at]
                comb[pl.ds((2 * l + s) * TILE, TILE), pl.ds(r * TILE, TILE)] = block.T

    def mirror(r):
        for l in range(4):
            for s in range(2):
                half = c if s == 0 else 1 - c
                rows, cols = pl.ds((2 * l + s) * TILE, TILE), pl.ds(r * TILE, TILE)
                other = own[l, y, half] if r == 0 else b2[r - 1, l, half]
                comb[rows, cols] = (2.0 * comb[rows, cols].astype(F32) - other.astype(F32)).astype(BF)

    turn(0)
    turn(1)
    service(1)
    turn(2)
    turn(3)
    mirror(0)
    service(2)
    for r in (1, 3, 2):
        arrive([y_copies[r]])
        mirror(r)

    def vectors_of(slot):
        return jnp.concatenate([ltb[slot, s, j] for j in range(4) for s in range(2)], axis=1)

    landed = {}

    def post(stage, n, region, copies):
        key = (stage, n % 4)
        settle(key)
        ssem, rsem = gs.at[stage, n % 4], gr.at[stage, n]
        for src, dst, target in copies:
            send(src, dst, ssem, rsem, target)
        pending[key] = landed[stage, n] = whole(region, ssem, rsem)

    def rows_of(n):
        return n // 2, pl.ds(*ROWS[n % 2])

    def stage_one(k):
        slots = ((NZ - k) % NZ, k + 1)
        for slot in slots:
            whole(ltb.at[slot, 1], cs.at[0, 0], cr.at[slot]).wait_recv()
        for half, slot in enumerate(slots):
            term = jnp.dot(vectors_of(slot), comb[...], preferred_element_type=F32).astype(BF)
            for r in range(NY):
                tbuf[k, half, r] = term[:, r * TILE : (r + 1) * TILE]
        for n in (2 * k, 2 * k + 1):
            _, rows = rows_of(n)
            if FORMS[k] == "E":
                post(0, n, r1.at[k, pl.ds(0, 4), rows],
                     [(tbuf.at[k, 1 - xo, :, rows], r1.at[k, pl.ds(0, 4), rows], across)])
            elif FORMS[k] == "G":
                post(0, n, r1.at[k, pl.ds(0, 6), rows],
                     [(tbuf.at[k, :, r, rows], r1.at[k, pl.ds(2 * (r - 1), 2), rows], y_down[r]) for r in (2, 1, 3)])
            else:
                post(0, n, r1.at[k, :, rows],
                     [(tbuf.at[k, 1 - xo, r, rows], r1.at[k, 3 + r, rows], y_slope[r]) for r in (2, 1, 3, 0)]
                     + [(tbuf.at[k, xo, r, rows], r1.at[k, r - 1, rows], y_down[r]) for r in (2, 1, 3)])

    def stage_two(n):
        k, rows = rows_of(n)
        landed[0, n].wait_recv()
        if FORMS[k] == "E":
            for r in range(NY):
                s2[k, r, rows] = (tbuf[k, xo, r, rows].astype(F32) + r1[k, r, rows].astype(F32)).astype(BF)
            post(1, n, r2.at[k, :, rows],
                 [(s2.at[k, r, rows], r2.at[k, r - 1, rows], y_down[r]) for r in (2, 1, 3)])
        elif FORMS[k] == "G":
            for h in range(2):
                total = tbuf[k, h, 0, rows].astype(F32)
                for r in range(1, NY):
                    total = total + r1[k, 2 * (r - 1) + h, rows].astype(F32)
                s2[k, h, rows] = total.astype(BF)
            post(1, n, r2.at[k, 0, rows], [(s2.at[k, 1 - xo, rows], r2.at[k, 0, rows], across)])
        else:
            total = tbuf[k, xo, 0, rows].astype(F32)
            for q in range(7):
                total = total + r1[k, q, rows].astype(F32)
            inter[k, xo, 0, rows] = total.astype(BF)
            mine = inter.at[k, xo, 0, rows]
            post(3, n, inter.at[k, 1 - xo, :, rows],
                 [(mine, inter.at[k, xo, r, rows], y_slant[r]) for r in (2, 1, 3, 0)])
            post(2, n, inter.at[k, xo, pl.ds(1, 3), rows],
                 [(mine, inter.at[k, xo, r, rows], y_up[r]) for r in (2, 1, 3)])

    def stage_three(n):
        k, rows = rows_of(n)
        landed[1, n].wait_recv()
        if FORMS[k] == "E":
            total = s2[k, 0, rows].astype(F32)
            for r in range(1, NY):
                total = total + r2[k, r - 1, rows].astype(F32)
            inter[k, xo, 0, rows] = total.astype(BF)
            post(2, n, inter.at[k, xo, pl.ds(1, 3), rows],
                 [(inter.at[k, xo, 0, rows], inter.at[k, xo, r, rows], y_up[r]) for r in (2, 1, 3)])
        else:
            inter[k, xo, 0, rows] = (s2[k, xo, rows].astype(F32) + r2[k, 0, rows].astype(F32)).astype(BF)
            post(2, n, inter.at[k, 1 - xo, 0, rows],
                 [(inter.at[k, xo, 0, rows], inter.at[k, xo, 0, rows], across)])

    def stage_four(n):
        k, rows = rows_of(n)
        landed[2, n].wait_recv()
        if FORMS[k] == "E":
            post(3, n, inter.at[k, 1 - xo, :, rows],
                 [(inter.at[k, xo, :, rows], inter.at[k, xo, :, rows], across)])
        else:
            post(3, n, inter.at[k, :, pl.ds(1, 3), rows],
                 [(inter.at[k, :, 0, rows], inter.at[k, :, r, rows], y_up[r]) for r in (2, 1, 3)])

    def finish(k):
        for n in (2 * k, 2 * k + 1):
            if FORMS[k] == "D":
                landed[2, n].wait_recv()
            landed[3, n].wait_recv()
        slots = ((NZ - k) % NZ, k + 1)
        pad = jnp.zeros((256 - 2 * BLOCK, TILE), BF)
        left = jnp.concatenate(
            [jnp.concatenate([inter[k, 0, r], inter[k, 1, r], pad], axis=0).T for r in range(NY)], axis=0
        )
        wide = jnp.zeros((256 - 2 * BLOCK, 8 * TILE), BF)
        right = jnp.concatenate([vectors_of(slots[0]), vectors_of(slots[1]), wide], axis=0)
        product = jnp.dot(left, right, preferred_element_type=F32)
        if k == 0:
            acc[...] = product
        else:
            acc[...] += product

    plan = []
    for step in range(3, 9):
        for u in range(4):
            plan.append((2 * (step - 2) + 0.5 * u - 0.3, 9, relay, (step, u)))
    for k in range(CHUNKS):
        short = FORMS[k] == "D"
        plan.append((2 * k, 4, stage_one, (k,)))
        for n in (2 * k, 2 * k + 1):
            plan.append((n + LAG, 3, stage_two, (n,)))
            if not short:
                plan.append((n + 2 * LAG, 2, stage_three, (n,)))
                plan.append((n + 3 * LAG, 1, stage_four, (n,)))
        plan.append((2 * k + 1 + (2 if short else 4) * LAG, 5, finish, (k,)))
    for _, _, act, what in sorted(plan, key=lambda item: item[:2]):
        act(*what)

    def conclude():
        turned = tops_of[...].T
        first = e_first[p // 2]
        sides = []
        for r in range(NY):
            at = (y + NY - r) % NY
            column = jnp.where(c == 0, turned[:, 0:1], turned[:, 1:2])
            for q in range(1, NY):
                choice = jnp.where(c == 0, turned[:, 2 * q : 2 * q + 1], turned[:, 2 * q + 1 : 2 * q + 2])
                column = jnp.where(at == q, choice, column)
            sides.append(column)
        for s in (1, 0):
            half = c if s == 0 else 1 - c
            tops = tops_of[pl.ds(2 * y + half, 1), :]
            for l in range(4):
                second = e_second[4 * xo + l]
                for r in range(NY):
                    at = (y + NY - r) % NY
                    values = (own[l, at, c] if s == 0 else pbuf[l, at]).astype(F32)
                    term = acc[r * TILE : (r + 1) * TILE, (2 * l + s) * TILE : (2 * l + s + 1) * TILE]
                    result = ((sides[r] + tops - first - second) * values + term).astype(BF)
                    if s == 0:
                        keep[l, at] = result
                    else:
                        away[l, at] = result
                if s == 0:
                    pltpu.make_async_copy(keep.at[l], out.at[l, :, c], lsem.at[5 + l]).start()
                else:
                    send(away.at[l], out.at[l, :, c], os_.at[0], or_.at[0], core)

    conclude()
    last = whole(away, os_.at[0], or_.at[0])
    arrive([last])

    def drain():
        for l in range(4):
            pltpu.make_async_copy(keep.at[l], out.at[l, :, c], lsem.at[5 + l]).wait()
        for copy in (x_all, p_copy, y_all, last, *pending.values()):
            copy.wait_send()

    drain()


def on_device(amplitudes, cholesky, energy_first, energy_second, energy_virtual):
    amp = amplitudes.reshape(4, NY, 2, TILE, TILE)
    chol = jnp.transpose(cholesky, (2, 0, 1))
    vmem = pl.BlockSpec(memory_space=pltpu.VMEM)
    hbm = pl.BlockSpec(memory_space=pltpu.HBM)
    dma = pltpu.SemaphoreType.DMA
    scratch = [
        pltpu.VMEM((4, NY, 2, TILE, TILE), BF),
        pltpu.VMEM((8, TILE), F32),
        pltpu.SMEM((32,), F32),
        pltpu.SMEM((8,), F32),
        pltpu.VMEM((SHARE, 8, TILE), BF),
        pltpu.VMEM((SHARE, 8, TILE), F32),
        pltpu.VMEM((2, 4 * SHARE, TILE), F32),
        pltpu.VMEM((2, 4 * SHARE, TILE), BF),
        pltpu.VMEM((NX, 4 * SHARE, TILE), BF),
        pltpu.VMEM((4, BLOCK, TILE), F32),
        pltpu.VMEM((NZ, 2, 4, BLOCK, TILE), BF),
        pltpu.VMEM((4, NY, TILE, TILE), BF),
        pltpu.VMEM((NY - 1, 4, 2, TILE, TILE), BF),
        pltpu.VMEM((8 * TILE, NY * TILE), BF),
        pltpu.VMEM((CHUNKS, 2, NY, BLOCK, TILE), BF),
        pltpu.VMEM((CHUNKS, 7, BLOCK, TILE), BF),
        pltpu.VMEM((CHUNKS, 4, BLOCK, TILE), BF),
        pltpu.VMEM((CHUNKS, 3, BLOCK, TILE), BF),
        pltpu.VMEM((CHUNKS, 2, NY, BLOCK, TILE), BF),
        pltpu.VMEM((NY * TILE, 8 * TILE), F32),
        pltpu.VMEM((4, NY, TILE, TILE), BF),
        pltpu.VMEM((4, NY, TILE, TILE), BF),
        dma((9,)), dma((1,)), dma((1,)), dma((1,)), dma((1,)), dma((1,)), dma((3,)),
        dma((2, 2)), dma((2, 8, 4)), dma((2, 2)), dma((NZ,)),
        dma((4, 4)), dma((4, 2 * CHUNKS)), dma((1,)), dma((1,)),
    ]
    result = pl.pallas_call(
        kernel,
        out_shape=jax.ShapeDtypeStruct(amp.shape, BF),
        in_specs=[hbm] * 5,
        out_specs=hbm,
        scratch_shapes=scratch,
        compiler_params=pltpu.CompilerParams(collective_id=0, has_side_effects=True, vmem_limit_bytes=GRANT),
        name="cycle",
    )(amp, chol, energy_first, energy_second, energy_virtual.reshape(8, TILE))
    return result.reshape(amplitudes.shape)


def solution(mesh):
    placed = (P("pair", None, "virt"), P(None, "virt", "pair"), P(), P(), P())
    return jax.shard_map(
        on_device, mesh=mesh, in_specs=placed, out_specs=P("pair", None, "virt"), check_vma=False
    )
```

```python
import jax
import jax.numpy as jnp
from jax import lax
from jax.experimental import pallas as pl
from jax.experimental.pallas import tpu as pltpu
from jax.sharding import PartitionSpec as P

MESH = pl.DeviceIdType.MESH
BF = jnp.bfloat16
F32 = jnp.float32
NZ, NX, NY = 16, 4, 4
TILE = 128
BLOCK = 112
SHARE = 28
CHUNKS = 8
FORMS = "EEGEEGED"
ROWS = ((0, 64), (64, 48))
LAG = 3
GRANT = 48 << 20


def kernel(amp, chol, first_hbm, second_hbm, virtual_hbm, out,
           own, tops_of, e_first, e_second, raw, wide_raw, flat, vec, xg, lay, ltb, pbuf, b2, comb, tbuf, r1, s2, r2, inter, acc, away,
           lsem, xs, xr, ps, pr, ys, yr, zs, zr, cs, cr, gs, gr, os_, or_):
    p = lax.axis_index("pair")
    v = lax.axis_index("virt")
    z, x, y, c = p // NX, p % NX, v // 2, v % 2
    xo = x % 2
    xp = x + 1 - 2 * xo

    def dev(z=z, x=x, y=y, c=c):
        return (z * NX + x, y * 2 + c)

    core = dev(c=1 - c)
    across = dev(x=xp)
    y_up = [None] + [dev(y=(y + r) % NY) for r in range(1, NY)]
    y_down = [None] + [dev(y=(y + NY - r) % NY) for r in range(1, NY)]
    x_up = [None] + [dev(x=(x + r) % NX) for r in range(1, NX)]
    z_up = dev(z=(z + 1) % NZ)
    z_down = dev(z=(z + NZ - 1) % NZ)

    y_slant = [across] + [dev(x=xp, y=(y + r) % NY) for r in range(1, NY)]
    y_slope = [across] + [dev(x=xp, y=(y + NY - r) % NY) for r in range(1, NY)]

    def send(src, dst, ssem, rsem, target):
        copy = pltpu.make_async_remote_copy(
            src_ref=src, dst_ref=dst, send_sem=ssem, recv_sem=rsem, device_id=target, device_id_type=MESH
        )
        copy.start()
        return copy

    def whole(ref, ssem, rsem):
        return pltpu.make_async_remote_copy(
            src_ref=ref, dst_ref=ref, send_sem=ssem, recv_sem=rsem, device_id=core, device_id_type=MESH
        )

    local = [
        pltpu.make_async_copy(amp, own, lsem.at[0]),
        pltpu.make_async_copy(virtual_hbm, tops_of, lsem.at[1]),
        pltpu.make_async_copy(first_hbm, e_first, lsem.at[2]),
        pltpu.make_async_copy(second_hbm, e_second, lsem.at[3]),
    ]
    chol_copy = pltpu.make_async_copy(chol, raw, lsem.at[4])
    chol_copy.start()
    for copy in local:
        copy.start()

    barrier = pltpu.get_barrier_semaphore()
    partners = [core, *y_up[1:], *x_up[1:], z_up, z_down, *y_slant[1:]]

    def enter():
        for partner in partners:
            pl.semaphore_signal(barrier, inc=1, device_id=partner, device_id_type=MESH)
        chol_copy.wait()
        wide_raw[...] = raw[...].astype(F32)
        for j in range(4):
            for g in range(2):
                flat[g, SHARE * j : SHARE * (j + 1), :] = wide_raw[:, 4 * g + j, :]
        for g in range(2):
            vec[g] = flat[g].astype(BF)
        pl.semaphore_wait(barrier, len(partners))

    enter()

    for r in range(1, NX):
        to = (x + r) % NX
        send(vec.at[to % 2], xg.at[x], xs.at[0], xr.at[0], x_up[r])
    p_copy = send(amp.at[:, :, 1 - c], pbuf, ps.at[0], pr.at[0], core)
    y_copies = [None] * NY
    for r in (1, 3, 2):
        y_copies[r] = send(amp.at[:, (y + r) % NY], b2.at[r - 1], ys.at[0], yr.at[r - 1], y_up[r])
    xg[x] = vec[xo]
    x_all = whole(xg.at[pl.ds(0, NX - 1)], xs.at[0], xr.at[0])
    y_all = whole(b2, ys.at[0], yr.at[0])

    def arrive(copies):
        for copy in copies:
            copy.wait_recv()

    def spread():
        for j in range(4):
            for k in range(NX):
                lay[j, SHARE * k : SHARE * (k + 1), :] = xg[k].astype(F32)[SHARE * j : SHARE * (j + 1), :]

    arrive([x_all])
    spread()

    z_copies = {}
    pending = {}

    def settle(key):
        if key in pending:
            pending.pop(key).wait_send()

    def share(way, step, u):
        slot = step if way == 0 else NZ - step
        key = ("c", way, step % 2)
        if u == 0:
            settle(key)
        sem = cs.at[way, step % 2]
        send(ltb.at[slot, 0, u], ltb.at[slot, 1, u], sem, cr.at[slot], core)
        pending[key] = whole(ltb.at[slot, 0], sem, cr.at[slot])

    def ring(step, way, u):
        if step > 8 - way:
            return
        source = step - 1 if way == 0 else (NZ + 1 - step) % NZ
        target = step if way == 0 else NZ - step
        key = ("z", way, step % 2)
        if u == 0:
            settle(key)
        sem = zs.at[way, step % 2]
        z_copies[way, step, u] = send(
            ltb.at[source, 0, u], ltb.at[target, 0, u], sem, zr.at[way, step - 1, u], z_up if way else z_down
        )
        pending[key] = whole(ltb.at[source, 0], sem, zr.at[way, step - 1, u])

    def relay(step, u):
        for way in range(2):
            if (way, step, u) in z_copies:
                z_copies[way, step, u].wait_recv()
                ring(step + 1, way, u)
                share(way, step, u)

    def service(step):
        for u in range(4):
            relay(step, u)

    for j in range(4):
        ltb[0, 0, j] = lay[j].astype(BF)
        ring(1, 0, j)
        ring(1, 1, j)
        share(0, 0, j)

    for copy in local:
        copy.wait()
    arrive([p_copy])

    def turn(r):
        at = (y + NY - r) % NY
        for l in range(4):
            for s in range(2):
                block = own[l, at, c] if s == 0 else pbuf[l, at]
                comb[pl.ds((2 * l + s) * TILE, TILE), pl.ds(r * TILE, TILE)] = block.T

    def mirror(r):
        for l in range(4):
            for s in range(2):
                half = c if s == 0 else 1 - c
                rows, cols = pl.ds((2 * l + s) * TILE, TILE), pl.ds(r * TILE, TILE)
                other = own[l, y, half] if r == 0 else b2[r - 1, l, half]
                comb[rows, cols] = (2.0 * comb[rows, cols].astype(F32) - other.astype(F32)).astype(BF)

    turn(0)
    turn(1)
    service(1)
    turn(2)
    turn(3)
    mirror(0)
    service(2)
    for r in (1, 3, 2):
        arrive([y_copies[r]])
        mirror(r)

    def vectors_of(slot):
        return jnp.concatenate([ltb[slot, s, j] for j in range(4) for s in range(2)], axis=1)

    landed = {}

    def post(stage, n, region, copies):
        key = (stage, n % 4)
        settle(key)
        ssem, rsem = gs.at[stage, n % 4], gr.at[stage, n]
        for src, dst, target in copies:
            send(src, dst, ssem, rsem, target)
        pending[key] = landed[stage, n] = whole(region, ssem, rsem)

    def rows_of(n):
        return n // 2, pl.ds(*ROWS[n % 2])

    def stage_one(k):
        slots = ((NZ - k) % NZ, k + 1)
        for slot in slots:
            whole(ltb.at[slot, 1], cs.at[0, 0], cr.at[slot]).wait_recv()
        for half, slot in enumerate(slots):
            term = jnp.dot(vectors_of(slot), comb[...], preferred_element_type=F32).astype(BF)
            for r in range(NY):
                tbuf[k, half, r] = term[:, r * TILE : (r + 1) * TILE]
        for n in (2 * k, 2 * k + 1):
            _, rows = rows_of(n)
            if FORMS[k] == "E":
                post(0, n, r1.at[k, pl.ds(0, 4), rows],
                     [(tbuf.at[k, 1 - xo, :, rows], r1.at[k, pl.ds(0, 4), rows], across)])
            elif FORMS[k] == "G":
                post(0, n, r1.at[k, pl.ds(0, 6), rows],
                     [(tbuf.at[k, :, r, rows], r1.at[k, pl.ds(2 * (r - 1), 2), rows], y_down[r]) for r in (2, 1, 3)])
            else:
                post(0, n, r1.at[k, :, rows],
                     [(tbuf.at[k, 1 - xo, r, rows], r1.at[k, 3 + r, rows], y_slope[r]) for r in (2, 1, 3, 0)]
                     + [(tbuf.at[k, xo, r, rows], r1.at[k, r - 1, rows], y_down[r]) for r in (2, 1, 3)])

    def stage_two(n):
        k, rows = rows_of(n)
        landed[0, n].wait_recv()
        if FORMS[k] == "E":
            for r in range(NY):
                s2[k, r, rows] = (tbuf[k, xo, r, rows].astype(F32) + r1[k, r, rows].astype(F32)).astype(BF)
            post(1, n, r2.at[k, :, rows],
                 [(s2.at[k, r, rows], r2.at[k, r - 1, rows], y_down[r]) for r in (2, 1, 3)])
        elif FORMS[k] == "G":
            for h in range(2):
                total = tbuf[k, h, 0, rows].astype(F32)
                for r in range(1, NY):
                    total = total + r1[k, 2 * (r - 1) + h, rows].astype(F32)
                s2[k, h, rows] = total.astype(BF)
            post(1, n, r2.at[k, 0, rows], [(s2.at[k, 1 - xo, rows], r2.at[k, 0, rows], across)])
        else:
            total = tbuf[k, xo, 0, rows].astype(F32)
            for q in range(7):
                total = total + r1[k, q, rows].astype(F32)
            inter[k, xo, 0, rows] = total.astype(BF)
            mine = inter.at[k, xo, 0, rows]
            post(3, n, inter.at[k, 1 - xo, :, rows],
                 [(mine, inter.at[k, xo, r, rows], y_slant[r]) for r in (2, 1, 3, 0)])
            post(2, n, inter.at[k, xo, pl.ds(1, 3), rows],
                 [(mine, inter.at[k, xo, r, rows], y_up[r]) for r in (2, 1, 3)])

    def stage_three(n):
        k, rows = rows_of(n)
        landed[1, n].wait_recv()
        if FORMS[k] == "E":
            total = s2[k, 0, rows].astype(F32)
            for r in range(1, NY):
                total = total + r2[k, r - 1, rows].astype(F32)
            inter[k, xo, 0, rows] = total.astype(BF)
            post(2, n, inter.at[k, xo, pl.ds(1, 3), rows],
                 [(inter.at[k, xo, 0, rows], inter.at[k, xo, r, rows], y_up[r]) for r in (2, 1, 3)])
        else:
            inter[k, xo, 0, rows] = (s2[k, xo, rows].astype(F32) + r2[k, 0, rows].astype(F32)).astype(BF)
            post(2, n, inter.at[k, 1 - xo, 0, rows],
                 [(inter.at[k, xo, 0, rows], inter.at[k, xo, 0, rows], across)])

    def stage_four(n):
        k, rows = rows_of(n)
        landed[2, n].wait_recv()
        if FORMS[k] == "E":
            post(3, n, inter.at[k, 1 - xo, :, rows],
                 [(inter.at[k, xo, :, rows], inter.at[k, xo, :, rows], across)])
        else:
            post(3, n, inter.at[k, :, pl.ds(1, 3), rows],
                 [(inter.at[k, :, 0, rows], inter.at[k, :, r, rows], y_up[r]) for r in (2, 1, 3)])

    def finish(k):
        for n in (2 * k, 2 * k + 1):
            if FORMS[k] == "D":
                landed[2, n].wait_recv()
            landed[3, n].wait_recv()
        slots = ((NZ - k) % NZ, k + 1)
        pad = jnp.zeros((256 - 2 * BLOCK, TILE), BF)
        left = jnp.concatenate(
            [jnp.concatenate([inter[k, 0, r], inter[k, 1, r], pad], axis=0).T for r in range(NY)], axis=0
        )
        wide = jnp.zeros((256 - 2 * BLOCK, 8 * TILE), BF)
        right = jnp.concatenate([vectors_of(slots[0]), vectors_of(slots[1]), wide], axis=0)
        product = jnp.dot(left, right, preferred_element_type=F32)
        if k == 0:
            acc[...] = product
        else:
            acc[...] += product

    plan = []
    for step in range(3, 9):
        for u in range(4):
            plan.append((2 * (step - 2) + 0.5 * u - 0.3, 9, relay, (step, u)))
    for k in range(CHUNKS):
        short = FORMS[k] == "D"
        plan.append((2 * k, 4, stage_one, (k,)))
        for n in (2 * k, 2 * k + 1):
            plan.append((n + LAG, 3, stage_two, (n,)))
            if not short:
                plan.append((n + 2 * LAG, 2, stage_three, (n,)))
                plan.append((n + 3 * LAG, 1, stage_four, (n,)))
        plan.append((2 * k + 1 + (2 if short else 4) * LAG, 5, finish, (k,)))
    for _, _, act, what in sorted(plan, key=lambda item: item[:2]):
        act(*what)

    def conclude():
        turned = tops_of[...].T
        first = e_first[p // 2]
        sides = []
        for r in range(NY):
            at = (y + NY - r) % NY
            column = jnp.where(c == 0, turned[:, 0:1], turned[:, 1:2])
            for q in range(1, NY):
                choice = jnp.where(c == 0, turned[:, 2 * q : 2 * q + 1], turned[:, 2 * q + 1 : 2 * q + 2])
                column = jnp.where(at == q, choice, column)
            sides.append(column)
        for s in (1, 0):
            half = c if s == 0 else 1 - c
            tops = tops_of[pl.ds(2 * y + half, 1), :]
            for l in range(4):
                second = e_second[4 * xo + l]
                for r in range(NY):
                    at = (y + NY - r) % NY
                    values = (own[l, at, c] if s == 0 else pbuf[l, at]).astype(F32)
                    term = acc[r * TILE : (r + 1) * TILE, (2 * l + s) * TILE : (2 * l + s + 1) * TILE]
                    result = ((sides[r] + tops - first - second) * values + term).astype(BF)
                    if s == 0:
                        out[l, at, c] = result
                    else:
                        away[l, at] = result
                if s == 1:
                    send(away.at[l], out.at[l, :, c], os_.at[0], or_.at[0], core)

    conclude()
    last = whole(away, os_.at[0], or_.at[0])
    arrive([last])

    def drain():
        for copy in (x_all, p_copy, y_all, last, *pending.values()):
            copy.wait_send()

    drain()


def on_device(amplitudes, cholesky, energy_first, energy_second, energy_virtual):
    amp = amplitudes.reshape(4, NY, 2, TILE, TILE)
    chol = jnp.transpose(cholesky, (2, 0, 1))
    vmem = pl.BlockSpec(memory_space=pltpu.VMEM)
    hbm = pl.BlockSpec(memory_space=pltpu.HBM)
    dma = pltpu.SemaphoreType.DMA
    scratch = [
        pltpu.VMEM((4, NY, 2, TILE, TILE), BF),
        pltpu.VMEM((8, TILE), F32),
        pltpu.SMEM((32,), F32),
        pltpu.SMEM((8,), F32),
        pltpu.VMEM((SHARE, 8, TILE), BF),
        pltpu.VMEM((SHARE, 8, TILE), F32),
        pltpu.VMEM((2, 4 * SHARE, TILE), F32),
        pltpu.VMEM((2, 4 * SHARE, TILE), BF),
        pltpu.VMEM((NX, 4 * SHARE, TILE), BF),
        pltpu.VMEM((4, BLOCK, TILE), F32),
        pltpu.VMEM((NZ, 2, 4, BLOCK, TILE), BF),
        pltpu.VMEM((4, NY, TILE, TILE), BF),
        pltpu.VMEM((NY - 1, 4, 2, TILE, TILE), BF),
        pltpu.VMEM((8 * TILE, NY * TILE), BF),
        pltpu.VMEM((CHUNKS, 2, NY, BLOCK, TILE), BF),
        pltpu.VMEM((CHUNKS, 7, BLOCK, TILE), BF),
        pltpu.VMEM((CHUNKS, 4, BLOCK, TILE), BF),
        pltpu.VMEM((CHUNKS, 3, BLOCK, TILE), BF),
        pltpu.VMEM((CHUNKS, 2, NY, BLOCK, TILE), BF),
        pltpu.VMEM((NY * TILE, 8 * TILE), F32),
        pltpu.VMEM((4, NY, TILE, TILE), BF),
        dma((5,)), dma((1,)), dma((1,)), dma((1,)), dma((1,)), dma((1,)), dma((3,)),
        dma((2, 2)), dma((2, 8, 4)), dma((2, 2)), dma((NZ,)),
        dma((4, 4)), dma((4, 2 * CHUNKS)), dma((1,)), dma((1,)),
    ]
    result = pl.pallas_call(
        kernel,
        out_shape=jax.ShapeDtypeStruct(amp.shape, BF),
        in_specs=[hbm] * 5,
        out_specs=vmem,
        scratch_shapes=scratch,
        compiler_params=pltpu.CompilerParams(collective_id=0, has_side_effects=True, vmem_limit_bytes=GRANT),
        name="cycle",
    )(*[pltpu.with_memory_space_constraint(a, pltpu.HBM)
        for a in (amp, chol, energy_first, energy_second, energy_virtual.reshape(8, TILE))])
    return result.reshape(amplitudes.shape)


def solution(mesh):
    placed = (P("pair", None, "virt"), P(None, "virt", "pair"), P(), P(), P())
    return jax.shard_map(
        on_device, mesh=mesh, in_specs=placed, out_specs=P("pair", None, "virt"), check_vma=False
    )
```
